256 devices in a mesh: phase: 16 (over y_hi, x, core), chan: 16 (over z, y_lo).
Axes of the slice: x: 4, y: 4 (y_hi: 2, y_lo: 2; y = y_hi * 2 + y_lo), z: 8, core: 2. Of those that a mesh axis runs over, the one named last changes fastest.
Arguments:
- frames: bfloat16 [64, 32, 2048], P(None, 'phase', 'chan'), may hold values from -6 to 6
- temporal_taps: float32 [4, 3, 64], replicated, may hold values from -3 to 3
- conv_weights: bfloat16 [4, 64, 27, 2, 64], P(None, None, None, None, 'chan'), may hold values from -0.15625 to 0.15625
- cotangent: bfloat16 [64, 32, 2048], P(None, 'phase', 'chan'), may hold values from -16 to 16
Outputs:
- final_frames: bfloat16 [64, 32, 2048], P(None, 'phase', 'chan')
- grad_frames: bfloat16 [64, 32, 2048], P(None, 'phase', 'chan')
- grad_taps: float32 [4, 3, 64], replicated
- grad_weights: float32 [4, 64, 27, 2, 64], P(None, None, None, None, 'chan')
The draws below stay inside these ranges and needn't reach their ends.
All inputs are finite; a program needn't handle non-finite values.
Results may differ from the reference program's by a relative error of at most 0.025.
Values may be sent and summed in bfloat16 or wider, within the bound.
No kernel may reach another device: no remote copies, remote signals or barrier semaphores. Data moves between devices by JAX's collectives and lax.ppermute only.
A program may use at most 64 MiB of HBM per device.

```python
import jax
import jax.numpy as jnp
from jax import lax

C = 64
BLOCKS = 4
SY = 8
SZ = 16
SX = 16
V = 2048
PHASES = 32


def draw_cotangent(key, part):
    base = jax.random.normal(key, (C, PHASES, V), jnp.float32)
    phase_pos = jnp.arange(PHASES, dtype=jnp.float32) / max(PHASES - 1, 1)
    plane_pos = (jnp.arange(V, dtype=jnp.int32) // (SY * SZ)).astype(jnp.float32) / max(SX - 1, 1)
    scale = 0.5 * (1.0 + 2.0 * phase_pos)[:, None] * (1.0 + 2.0 * plane_pos)[None, :]
    return jnp.clip(base * scale[None, :, :], -16.0, 16.0).astype(jnp.bfloat16)


def shard_levels(key, extent, pieces, smallest, high):
    def one(dim, shards_of):
        heights = jax.random.uniform(jax.random.fold_in(jax.random.fold_in(key, 6), dim), (shards_of,), jnp.float32, smallest / len(pieces), high / len(pieces))
        return jnp.repeat(jnp.exp(heights), extent[dim] // shards_of).reshape((-1,) + (1,) * (len(extent) - dim - 1))

    gain = one(*pieces[0])
    for cut in pieces[1:]:
        gain = gain * one(*cut)
    return gain


def bell_draw(key, shape, scale, most, cuts=(), kind=jnp.bfloat16):
    array = jax.random.normal(key, shape, jnp.float32) * scale
    if len(cuts) > 0:
        array = shard_levels(key, shape, cuts, -0.22, 0.18) * array
    return jnp.clip(array, min=-most, max=most).astype(kind)


def setup_inputs(seed: int = 0) -> dict:
    splits = jax.random.split(jax.random.key(seed), 5)
    frames = bell_draw(splits[0], (C, PHASES, V), 1.0, 6.0, ((1, 16), (2, 16)))
    temporal_taps = bell_draw(splits[1], (BLOCKS, 3, C), 0.6, 3.0, (), jnp.float32)
    conv_weights = bell_draw(splits[2], (BLOCKS, C, 27, 2, C), (27 * C) ** -0.5, 0.15625, ((4, 16),))
    cotangent = draw_cotangent(jax.random.fold_in(splits[4], 71), 0)
    return dict(frames=frames, temporal_taps=temporal_taps, conv_weights=conv_weights, cotangent=cotangent)


def conv_cells(mixed, kernel):
    chans = mixed.shape[0]
    phases = mixed.shape[1]
    lhs = jnp.transpose(mixed, (1, 0, 2)).reshape(phases, chans, SX, SY, SZ)
    kern = kernel.reshape(chans, 3, 3, 3, 2 * chans)
    kern = jnp.transpose(kern, (4, 0, 1, 2, 3))
    result = lax.conv_general_dilated(lhs, kern, (1, 1, 1), [(1, 1), (1, 1), (1, 1)], dimension_numbers=('NCDHW', 'OIDHW', 'NCDHW'), precision=lax.Precision.HIGHEST)
    result = result.reshape(phases, 2, chans, SX * SY * SZ)
    return jnp.transpose(result, (2, 1, 0, 3))

def reference(frames, temporal_taps, conv_weights, cotangent):
    state = frames
    saved = []
    for block_num in range(BLOCKS):
        reach = 2 ** block_num
        behind = jnp.roll(state, reach, axis=1)
        ahead = jnp.roll(state, -reach, axis=1)
        tap_rows = temporal_taps[block_num][:, :, None, None]
        mixed = (tap_rows[0] * behind.astype(jnp.float32) + tap_rows[1] * state.astype(jnp.float32) + tap_rows[2] * ahead.astype(jnp.float32)).astype(jnp.bfloat16)
        conv_out = conv_cells(mixed.astype(jnp.float32), conv_weights[block_num].astype(jnp.float32))
        value_part = conv_out[:, 0]
        gate_sig = jax.nn.sigmoid(conv_out[:, 1])
        saved.append((state, behind, ahead, mixed, value_part, gate_sig))
        state = (state.astype(jnp.float32) + value_part * gate_sig).astype(jnp.bfloat16)
    grad_state = cotangent
    weight_grads = [None] * BLOCKS
    tap_grads = [None] * BLOCKS
    for block_num in reversed(range(BLOCKS)):
        reach = 2 ** block_num
        prior, behind, ahead, mixed, value_part, gate_sig = saved[block_num]
        tap_rows = temporal_taps[block_num][:, :, None, None]
        grad_y = grad_state.astype(jnp.float32)
        grad_z = jnp.stack([grad_y * gate_sig, grad_y * value_part * gate_sig * (1.0 - gate_sig)], axis=1).astype(jnp.bfloat16)
        outputs_now, pullback = jax.vjp(conv_cells, mixed.astype(jnp.float32), conv_weights[block_num].astype(jnp.float32))
        grad_mix, grad_kernel = pullback(grad_z.astype(jnp.float32))
        grad_tap = jnp.stack([lax.optimization_barrier(jnp.sum(grad_mix * behind.astype(jnp.float32), axis=(1, 2))), lax.optimization_barrier(jnp.sum(grad_mix * prior.astype(jnp.float32), axis=(1, 2))), lax.optimization_barrier(jnp.sum(grad_mix * ahead.astype(jnp.float32), axis=(1, 2)))])
        grad_low = grad_mix.astype(jnp.bfloat16).astype(jnp.float32)
        grad_state = (grad_y + tap_rows[0] * jnp.roll(grad_low, -reach, axis=1) + tap_rows[1] * grad_low + tap_rows[2] * jnp.roll(grad_low, reach, axis=1)).astype(jnp.bfloat16)
        weight_grads[block_num] = grad_kernel
        tap_grads[block_num] = grad_tap
    return (state, grad_state, jnp.stack(tap_grads), jnp.stack(weight_grads))
```

```python
import functools

import jax
import jax.numpy as jnp
from jax import lax
from jax.experimental import pallas as pl
from jax.experimental.pallas import tpu as pltpu
from jax.sharding import PartitionSpec as P


BLOCKS = 4
SY = 8
SZ = 16
CELLS = SY * SZ
CHANS = 64
OFFSETS = 27
DEPTH = OFFSETS * CHANS
f32 = jnp.float32
bf16 = jnp.bfloat16


def call(body, out_shape, *args, scratch=(), flops=1_000_000, room=12):
    size = sum(a.size * a.dtype.itemsize for a in args)
    return pl.pallas_call(
        body,
        out_shape=out_shape,
        scratch_shapes=list(scratch),
        compiler_params=pltpu.CompilerParams(vmem_limit_bytes=room << 20),
        cost_estimate=pl.CostEstimate(flops=flops, bytes_accessed=size, transcendentals=0),
    )(*args)


def shaped(shape, kind):
    return jax.ShapeDtypeStruct(shape, kind)


def inside_masks(sign):
    places = lax.broadcasted_iota(jnp.int32, (1, CELLS), 1)
    masks = []
    for kk in range(9):
        dy, dz = sign * (kk // 3 - 1), sign * (kk % 3 - 1)
        y, z = places // SZ + dy, places % SZ + dz
        masks.append((y >= 0) & (y < SY) & (z >= 0) & (z < SZ))
    return masks


def spread_unit(unit, masks, sign):
    wide = unit.astype(f32)
    pieces = []
    for kk in range(9):
        step = sign * ((kk // 3 - 1) * SZ + kk % 3 - 1)
        if step == 0:
            pieces.append(unit)
        else:
            moved = pltpu.roll(wide, (-step) % CELLS, 1)
            pieces.append(jnp.where(masks[kk], moved, 0.0).astype(bf16))
    return pieces


def fill_columns(columns, planes, sign):
    masks = inside_masks(sign)
    rows = planes[0][0].shape[0]
    for dx in range(3):
        source = planes[dx] if sign > 0 else planes[2 - dx]
        for t, unit in enumerate(source):
            for kk, piece in enumerate(spread_unit(unit, masks, sign)):
                start = (dx * 9 + kk) * rows
                columns[start : start + rows, t * CELLS : (t + 1) * CELLS] = piece


def sort_matrix(transposed):
    r = lax.broadcasted_iota(jnp.int32, (128, 128), 0)
    c = lax.broadcasted_iota(jnp.int32, (128, 128), 1)
    if transposed:
        r, c = c, r
    wanted = (r % 64) // 4 * 8 + r // 64 * 4 + r % 4
    return jnp.where(c == wanted, 1.0, 0.0).astype(bf16)


def sort_kernel(raw, out):
    order = sort_matrix(False)
    for n in range(2):
        rows = raw[:, 8 * n : 8 * n + 8, :].reshape(128, DEPTH)
        out[n] = jnp.dot(order, rows, preferred_element_type=f32).astype(bf16)


def flip_kernel(weights, out):
    r = lax.broadcasted_iota(jnp.int32, (CHANS, CHANS), 0)
    c = lax.broadcasted_iota(jnp.int32, (CHANS, CHANS), 1)
    eye = jnp.where(r == c, 1.0, 0.0).astype(bf16)
    for n in range(2):
        for k in range(OFFSETS):
            piece = weights[n, :, k * CHANS : (k + 1) * CHANS]
            turned = lax.dot_general(
                eye, piece, (((1,), (1,)), ((), ())), preferred_element_type=f32
            )
            out[n, :, k * 128 : (k + 1) * 128] = turned.astype(bf16)


def tap_columns(taps, block):
    return [taps[:, 3 * block + n : 3 * block + n + 1] for n in range(3)]


def mix(t, before, now, after):
    total = t[0] * before.astype(f32) + t[1] * now.astype(f32) + t[2] * after.astype(f32)
    return total.astype(bf16)


def mix_kernel(block, taps, state, behind, ahead, out):
    t = tap_columns(taps, block)
    for n in range(2):
        out[n] = mix(t, behind[n], state[n], ahead[n])


def front_mix_kernel(taps, own, back1, next1, back2, next2, mixed, line):
    t = tap_columns(taps, 0)
    for x in range(5):
        f = [back2[x, 0], back1[x, 0], back1[x, 1], own[x, 0], own[x, 1]]
        f += [next1[x, 0], next1[x, 1], next2[x, 0]]
        for q in range(6):
            mixed[x, q] = mix(t, f[q], f[q + 1], f[q + 2])
        if x == 2:
            for q in range(4):
                line[q] = f[q + 2]


def gated_sum(conv, n):
    v = conv[:CHANS, n * CELLS : (n + 1) * CELLS]
    s = jax.nn.sigmoid(conv[CHANS:, n * CELLS : (n + 1) * CELLS])
    return v, s


def front_kernel(
    edge, taps, weights, mixed, own, back1, next1,
    value0, gate0, line1, mixed1, value1, gate1, after, columns, narrow,
):
    masks = inside_masks(1)
    for x in range(5):
        for q in range(6):
            for kk, piece in enumerate(spread_unit(mixed[x, q], masks, 1)):
                columns[x, kk * CHANS : (kk + 1) * CHANS, q * CELLS : (q + 1) * CELLS] = piece
    t = tap_columns(taps, 1)
    third = 9 * CHANS
    planes = []
    for x in range(3):
        conv = jnp.zeros((2 * CHANS, 6 * CELLS), f32)
        for dx in range(3):
            conv = conv + jnp.dot(
                weights[0, :, dx * third : (dx + 1) * third],
                columns[x + dx],
                preferred_element_type=f32,
            )
        f = [back1[x + 1, 0], back1[x + 1, 1], own[x + 1, 0], own[x + 1, 1]]
        f += [next1[x + 1, 0], next1[x + 1, 1]]
        states = []
        for q in range(6):
            v, s = gated_sum(conv, q)
            state = f[q].astype(f32) + v * s
            if x == 1:
                state = state.astype(bf16)
                line1[q] = state
                if q in (2, 3):
                    value0[q - 2] = v
                    gate0[q - 2] = s
            else:
                flag = edge[x // 2 : x // 2 + 1, :] > 0.5
                state = jnp.where(flag, state, 0.0).astype(bf16)
            states.append(state)
        units = [mix(t, states[n], states[n + 2], states[n + 4]) for n in range(2)]
        for n in range(2):
            mixed1[x, n] = units[n]
        planes.append(units)
    fill_columns(narrow, planes, 1)
    conv = jnp.dot(weights[1], narrow[...], preferred_element_type=f32)
    for n in range(2):
        v, s = gated_sum(conv, n)
        value1[n] = v
        gate1[n] = s
        after[n] = (line1[n + 2].astype(f32) + v * s).astype(bf16)


def conv_kernel(which, weights, mixed, left, right, state, *rest):
    fill_columns(rest[-1], [[a[0], a[1]] for a in (left, mixed, right)], 1)
    conv = jnp.dot(weights[which], rest[-1][...], preferred_element_type=f32)
    for n in range(2):
        v, s = gated_sum(conv, n)
        after = (state[n].astype(f32) + v * s).astype(bf16)
        if which == 0:
            rest[0][n] = v
            rest[1][n] = s
            rest[2][n] = after
        else:
            rest[1][n, :CHANS], rest[1][n, CHANS:] = gated(rest[0][n].astype(f32), v, s)
            rest[2][n] = after


def gated(y, v, s):
    return (y * s).astype(bf16), (y * v * s * (1.0 - s)).astype(bf16)


def whole_line(block, line):
    shift = min(2**block, 2)
    if len(line) == 1:
        units = [line[0][n] for n in range(2 + 2 * shift)]
    else:
        units = [ref[n] for ref in line for n in range(2)]
    return shift, units


def data_kernel(block, weight, gz, left, right, *rest):
    line, (low, tap, columns) = rest[:-3], rest[-3:]
    fill_columns(columns, [[a[0], a[1]] for a in (left, gz, right)], -1)
    grad = jnp.dot(weight[block % 2], columns[...], preferred_element_type=f32)
    shift, units = whole_line(block, line)
    totals = [0.0, 0.0, 0.0]
    for n in range(2):
        m = grad[:, n * CELLS : (n + 1) * CELLS]
        low[n] = m.astype(bf16)
        for which in range(3):
            totals[which] = totals[which] + m * units[n + which * shift].astype(f32)
    for which in range(3):
        tap[:, which : which + 1] = jnp.sum(totals[which], axis=1, keepdims=True)


def weight_kernel(offsets, gz, *rest):
    sources, (out, columns) = rest[:-2], rest[-2:]
    if len(sources) == 1:
        x, t = offsets
        planes = [[sources[0][x + n, t], sources[0][x + n, t + 1]] for n in range(3)]
    else:
        planes = [[a[0], a[1]] for a in sources]
    fill_columns(columns, planes, 1)
    both = jnp.concatenate([gz[0], gz[1]], axis=1)
    both = jnp.dot(sort_matrix(True), both, preferred_element_type=f32).astype(bf16)
    grad = lax.dot_general(
        columns[...], both, (((1,), (1,)), ((), ())), preferred_element_type=f32
    )
    out[:13] = grad[: 13 * 128].astype(bf16).reshape(13, 128, 128)
    out[13, :CHANS] = grad[13 * 128 :].astype(bf16)
    out[13, CHANS:] = jnp.zeros((CHANS, 128), bf16)
    out[14:] = jnp.zeros((2, 128, 128), bf16)


def turned_sum(pieces, start):
    total = pieces[0, start : start + 128].astype(f32)
    for n in range(1, 16):
        total = total + pieces[n, start : start + 128].astype(f32)
    r = lax.broadcasted_iota(jnp.int32, (128, 128), 0)
    c = lax.broadcasted_iota(jnp.int32, (128, 128), 1)
    eye = jnp.where(r == c, 1.0, 0.0).astype(bf16)
    swapped = lax.dot_general(
        eye, total.astype(bf16), (((1,), (1,)), ((), ())), preferred_element_type=f32
    )
    return swapped.astype(bf16)


def part_kernel(pieces, out):
    for n in range(3):
        out[2 - n] = turned_sum(pieces, 128 * n)


def halves(value):
    high = value.astype(bf16)
    low = (value - high.astype(f32)).astype(bf16)
    return high, low


def pack_kernel(pieces, later, taps, out):
    parts = [turned_sum(pieces, 0), later[0], later[1], later[2]]
    high, low = halves(taps[...])
    for j in range(16):
        for b in range(BLOCKS):
            out[j, 8 * b : 8 * b + 8] = parts[b][8 * j : 8 * j + 8]
        out[j, 32:40] = high
        out[j, 40:48] = low


def repack_kernel(pieces, out):
    total = pieces[0].astype(f32)
    for n in range(1, 16):
        total = total + pieces[n].astype(f32)
    high, low = halves(total[32:40] + total[40:48])
    grads = total[:32].astype(bf16)
    for p in range(16):
        out[p, :32] = grads
        out[p, 32:40] = high
        out[p, 40:48] = low


def back_state(block, taps, grad, low, behind, ahead):
    shift, units = whole_line(block, (behind, low, ahead)) if block else (1, None)
    if block == 0:
        units = [behind[0], low[0], low[1], ahead[0]]
    t = tap_columns(taps, block)
    return [
        (
            grad[n].astype(f32)
            + t[0] * units[n + 2 * shift].astype(f32)
            + t[1] * units[n + shift].astype(f32)
            + t[2] * units[n].astype(f32)
        ).astype(bf16)
        for n in range(2)
    ]


def last_kernel(block, taps, grad, low, behind, ahead, out):
    for n, g in enumerate(back_state(block, taps, grad, low, behind, ahead)):
        out[n] = g


def step_kernel(block, taps, grad, low, behind, ahead, value, gate, out, gz):
    for n, g in enumerate(back_state(block, taps, grad, low, behind, ahead)):
        out[n] = g
        a, b = gated(g.astype(f32), value[n], gate[n])
        gz[n, :CHANS] = a
        gz[n, CHANS:] = b


def beside(cells, axis, distance):
    count = lax.axis_size(axis)
    pairs = [(i, i + distance) for i in range(count) if 0 <= i + distance < count]
    return lax.ppermute(cells, axis, pairs)


def sides(cells, axis):
    return beside(cells, axis, 1), beside(cells, axis, -1)


def turned(block, distance):
    count = lax.axis_size("phase")
    return lax.ppermute(block, "phase", [((i - distance) % count, i) for i in range(count)])


def neighbours(source, reach):
    if reach == 1:
        return turned(source[1:], 1), turned(source[:1], -1)
    return turned(source, reach // 2), turned(source, -(reach // 2))


def spread(piece, axis):
    count = lax.axis_size(axis)
    copies = jnp.broadcast_to(piece[None], (count,) + piece.shape)
    return lax.all_to_all(copies, axis, 0, 0, tiled=True)


def per_device(frames, temporal_taps, conv_weights, cotangent):
    groups = lax.axis_size("chan")
    own = CHANS // groups
    rows = jnp.transpose(conv_weights, (0, 3, 4, 2, 1)).reshape(BLOCKS, 2 * own, DEPTH)
    taps = temporal_taps.reshape(3 * BLOCKS, CHANS).T
    unit = (2, CHANS, CELLS)
    gunit = (2, 2 * CHANS, CELLS)
    state = jnp.transpose(frames, (1, 0, 2))
    grad = jnp.transpose(cotangent, (1, 0, 2))
    columns = pltpu.VMEM((DEPTH, 2 * CELLS), bf16)
    wide_columns = pltpu.VMEM((2 * DEPTH, 2 * CELLS), bf16)
    place = lax.axis_index("chan")
    edge = jnp.stack([place > 0, place < groups - 1]).astype(f32)
    edge = jnp.broadcast_to(edge[:, None], (2, CELLS))

    raw = []
    for n in range(2):
        raw.append(spread(rows[2 * n : 2 * n + 2].reshape(4 * own, DEPTH), "chan"))
    weights = [call(sort_kernel, shaped((2, 128, DEPTH), bf16), r) for r in raw]

    cells = [beside(state, "chan", d) for d in (2, 1, -1, -2)]
    here = jnp.stack([cells[0], cells[1], state, cells[2], cells[3]])
    back1, next1 = turned(here, 1), turned(here, -1)
    back2, next2 = turned(here[:, 1:], 2), turned(here[:, :1], -2)
    mixed0, line0 = call(
      front_mix_kernel,
      [shaped((5, 6, CHANS, CELLS), bf16), shaped((4, CHANS, CELLS), bf16)],
      taps, here, back1, next1, back2, next2,
    )
    value0, gate0, line1, mixed1, value1, gate1, state = call(
        front_kernel,
        [
            shaped(unit, f32),
            shaped(unit, f32),
            shaped((6, CHANS, CELLS), bf16),
            shaped((3, 2, CHANS, CELLS), bf16),
            shaped(unit, f32),
            shaped(unit, f32),
            shaped(unit, bf16),
        ],
        edge, taps, weights[0], mixed0, here, back1, next1,
        scratch=[pltpu.VMEM((5, 9 * CHANS, 6 * CELLS), bf16), columns],
    )
    saved = [
        ((line0,), (mixed0,), (1, 2), value0, gate0),
        ((line1,), (mixed1,), (0, 0), value1, gate1),
    ]
    for b in range(2, BLOCKS):
        prior = state
        behind, ahead = neighbours(state, 2**b)
        mixed = call(
            functools.partial(mix_kernel, b), shaped(unit, bf16), taps, state, behind, ahead
        )
        left, right = sides(mixed, "chan")
        if b < BLOCKS - 1:
            value, gate, state = call(
                functools.partial(conv_kernel, 0),
                [shaped(unit, f32), shaped(unit, f32), shaped(unit, bf16)],
                weights[1], mixed, left, right, state,
                scratch=[columns],
            )
            saved.append(((behind, prior, ahead), (left, mixed, right), None, value, gate))
        else:
            gz, state = call(
                functools.partial(conv_kernel, 1),
                [shaped(gunit, bf16), shaped(unit, bf16)],
                weights[1], mixed, left, right, state, grad,
                scratch=[columns],
            )
            saved.append(((behind, prior, ahead), (left, mixed, right), None, None, None))
    final = state
    backs = [call(flip_kernel, shaped((2, CHANS, 2 * DEPTH), bf16), w) for w in weights]

    held = []
    tap_grads = [None] * BLOCKS
    for b in reversed(range(BLOCKS)):
        line, mixed, offsets, _, _ = saved[b]
        gleft, gright = sides(gz, "chan")
        pieces = call(
            functools.partial(weight_kernel, offsets),
            shaped((16, 128, 128), bf16),
            gz, *mixed,
            scratch=[columns],
        )
        held.append(pieces)
        if b == 1:
            early = jnp.concatenate(held, axis=1)
            early = lax.all_to_all(early, "phase", 0, 0, tiled=True)
        if b == 0:
            late = lax.all_to_all(pieces, "phase", 0, 0, tiled=True)
        low, tap_grads[b] = call(
            functools.partial(data_kernel, b),
            [shaped(unit, bf16), shaped((CHANS, 3), f32)],
            backs[b // 2], gz, gleft, gright, *line,
            scratch=[wide_columns],
        )
        behind, ahead = neighbours(low, 2**b)
        if b == 0:
            grad = call(
                functools.partial(last_kernel, b),
                shaped(unit, bf16),
                taps, grad, low, behind, ahead,
            )
        else:
            grad, gz = call(
                functools.partial(step_kernel, b),
                [shaped(unit, bf16), shaped(gunit, bf16)],
                taps, grad, low, behind, ahead, saved[b - 1][3], saved[b - 1][4],
            )
    parts = call(part_kernel, shaped((3, 128, 128), bf16), early)
    tap_rows = jnp.concatenate(tap_grads, axis=1).T.reshape(6, 2 * CHANS)
    tap_rows = jnp.pad(tap_rows, [(0, 2), (0, 0)])
    packed = call(pack_kernel, shaped((16, 48, 128), bf16), late, parts, tap_rows)
    packed = lax.all_to_all(packed, "chan", 0, 0, tiled=True)
    packed = call(repack_kernel, shaped((16, 48, 128), bf16), packed)
    packed = lax.all_to_all(packed, "phase", 0, 0, tiled=True)
    grad_rows = packed[:14, :32].astype(f32).reshape(14, BLOCKS, 2, own, 2, CHANS)
    grad_rows = jnp.transpose(grad_rows, (1, 5, 0, 4, 2, 3)).reshape(BLOCKS, CHANS, 28, 2, own)
    grad_weights = grad_rows[:, :, :OFFSETS]
    grad_taps = jnp.sum(packed[:, 32:].astype(f32), axis=0)
    grad_taps = (grad_taps[:6] + grad_taps[8:14]).reshape(BLOCKS, 3, CHANS)
    return (
        jnp.transpose(final, (1, 0, 2)),
        jnp.transpose(grad, (1, 0, 2)),
        grad_taps,
        grad_weights,
    )


def solution(mesh):
    in_specs = (
        P(None, "phase", "chan"),
        P(),
        P(None, None, None, None, "chan"),
        P(None, "phase", "chan"),
    )
    out_specs = (
        P(None, "phase", "chan"),
        P(None, "phase", "chan"),
        P(),
        P(None, None, None, None, "chan"),
    )
    return jax.shard_map(
        per_device, mesh=mesh, in_specs=in_specs, out_specs=out_specs, check_vma=False
    )
```

```python
import functools

import jax
import jax.numpy as jnp
from jax import lax
from jax.experimental import pallas as pl
from jax.experimental.pallas import tpu as pltpu
from jax.sharding import PartitionSpec as P


BLOCKS = 4
SY = 8
SZ = 16
CELLS = SY * SZ
CHANS = 64
OFFSETS = 27
DEPTH = OFFSETS * CHANS
f32 = jnp.float32
bf16 = jnp.bfloat16


def call(body, out_shape, *args, scratch=(), flops=1_000_000, room=12):
    size = sum(a.size * a.dtype.itemsize for a in args)
    return pl.pallas_call(
        body,
        out_shape=out_shape,
        scratch_shapes=list(scratch),
        compiler_params=pltpu.CompilerParams(vmem_limit_bytes=room << 20),
        cost_estimate=pl.CostEstimate(flops=flops, bytes_accessed=size, transcendentals=0),
    )(*args)


def shaped(shape, kind):
    return jax.ShapeDtypeStruct(shape, kind)


def inside_masks(sign):
    places = lax.broadcasted_iota(jnp.int32, (1, CELLS), 1)
    masks = []
    for kk in range(9):
        dy, dz = sign * (kk // 3 - 1), sign * (kk % 3 - 1)
        y, z = places // SZ + dy, places % SZ + dz
        masks.append((y >= 0) & (y < SY) & (z >= 0) & (z < SZ))
    return masks


def spread_unit(unit, masks, sign):
    wide = unit.astype(f32)
    pieces = []
    for kk in range(9):
        step = sign * ((kk // 3 - 1) * SZ + kk % 3 - 1)
        if step == 0:
            pieces.append(unit)
        else:
            moved = pltpu.roll(wide, (-step) % CELLS, 1)
            pieces.append(jnp.where(masks[kk], moved, 0.0).astype(bf16))
    return pieces


def fill_columns(columns, planes, sign):
    masks = inside_masks(sign)
    rows = planes[0][0].shape[0]
    for dx in range(3):
        source = planes[dx] if sign > 0 else planes[2 - dx]
        for t, unit in enumerate(source):
            for kk, piece in enumerate(spread_unit(unit, masks, sign)):
                start = (dx * 9 + kk) * rows
                columns[start : start + rows, t * CELLS : (t + 1) * CELLS] = piece


def permutation(wanted):
    r = lax.broadcasted_iota(jnp.int32, (128, 128), 0)
    c = lax.broadcasted_iota(jnp.int32, (128, 128), 1)
    return jnp.where(wanted(r) == c, 1.0, 0.0).astype(bf16)


def sort_kernel(half, odd, mine, other, out):
    order = permutation(lambda r: r % 64 // 4 * 8 + r // 64 * 4 + r % 4)
    keep = (odd[:1, :1] > 0.5) if half else (odd[:1, :1] < 0.5)
    for n in range(2):
        here = mine[:, 8 * n : 8 * n + 8, :].reshape(128, DEPTH)
        there = other[:, 8 * n : 8 * n + 8, :].reshape(128, DEPTH)
        rows = jnp.where(keep, here.astype(f32), there.astype(f32)).astype(bf16)
        out[n] = jnp.dot(order, rows, preferred_element_type=f32).astype(bf16)


def flip_kernel(weights, out):
    r = lax.broadcasted_iota(jnp.int32, (CHANS, CHANS), 0)
    c = lax.broadcasted_iota(jnp.int32, (CHANS, CHANS), 1)
    eye = jnp.where(r == c, 1.0, 0.0).astype(bf16)
    for n in range(2):
        for k in range(OFFSETS):
            piece = weights[n, :, k * CHANS : (k + 1) * CHANS]
            turned = lax.dot_general(
                eye, piece, (((1,), (1,)), ((), ())), preferred_element_type=f32
            )
            out[n, :, k * 128 : (k + 1) * 128] = turned.astype(bf16)


def tap_columns(taps, block):
    return [taps[:, 3 * block + n : 3 * block + n + 1] for n in range(3)]


def mix(t, before, now, after):
    total = t[0] * before.astype(f32) + t[1] * now.astype(f32) + t[2] * after.astype(f32)
    return total.astype(bf16)


def mix_kernel(block, taps, state, behind, ahead, out):
    t = tap_columns(taps, block)
    for n in range(2):
        out[n] = mix(t, behind[n], state[n], ahead[n])


def wide_columns(columns, planes):
    masks = inside_masks(1)
    for x, units in enumerate(planes):
        for q, unit in enumerate(units):
            for kk, piece in enumerate(spread_unit(unit, masks, 1)):
                columns[x, kk * CHANS : (kk + 1) * CHANS, q * CELLS : (q + 1) * CELLS] = piece


def wide_conv(weight, columns, x):
    third = 9 * CHANS
    total = None
    for dx in range(3):
        part = jnp.dot(
            weight[:, dx * third : (dx + 1) * third], columns[x + dx], preferred_element_type=f32
        )
        total = part if dx == 0 else total + part
    return total


def front_mix_kernel(taps, *refs):
    planes, (mixed, line) = refs[:5], refs[5:]
    t = tap_columns(taps, 0)
    for x in range(5):
        for q in range(6):
            mixed[x, q] = mix(t, planes[x][q], planes[x][q + 1], planes[x][q + 2])
    for q in range(4):
        line[q] = planes[2][q + 2]


def gated_sum(conv, n):
    v = conv[:CHANS, n * CELLS : (n + 1) * CELLS]
    s = jax.nn.sigmoid(conv[CHANS:, n * CELLS : (n + 1) * CELLS])
    return v, s


def front_kernel(
    edge, taps, weights, mixed, before, own, after_own,
    value0, gate0, line1, mixed1, value1, gate1, after, columns, narrow,
):
    wide_columns(columns, [[mixed[x, q] for q in range(6)] for x in range(5)])
    t = tap_columns(taps, 1)
    planes = []
    for x in range(3):
        conv = wide_conv(weights[0], columns, x)
        f = (before, own, after_own)[x]
        states = []
        for q in range(6):
            v, s = gated_sum(conv, q)
            state = f[q + 1].astype(f32) + v * s
            if x == 1:
                state = state.astype(bf16)
                line1[q] = state
                if q in (2, 3):
                    value0[q - 2] = v
                    gate0[q - 2] = s
            else:
                flag = edge[x // 2 : x // 2 + 1, :] > 0.5
                state = jnp.where(flag, state, 0.0).astype(bf16)
            states.append(state)
        units = [mix(t, states[n], states[n + 2], states[n + 4]) for n in range(2)]
        for n in range(2):
            mixed1[x, n] = units[n]
        planes.append(units)
    fill_columns(narrow, planes, 1)
    conv = jnp.dot(weights[1], narrow[...], preferred_element_type=f32)
    for n in range(2):
        v, s = gated_sum(conv, n)
        value1[n] = v
        gate1[n] = s
        after[n] = (line1[n + 2].astype(f32) + v * s).astype(bf16)


def conv_kernel(weights, mixed, left, right, state, value, gate, after, columns):
    fill_columns(columns, [[a[0], a[1]] for a in (left, mixed, right)], 1)
    conv = jnp.dot(weights[0], columns[...], preferred_element_type=f32)
    for n in range(2):
        v, s = gated_sum(conv, n)
        value[n] = v
        gate[n] = s
        after[n] = (state[n].astype(f32) + v * s).astype(bf16)


def turn_kernel(weights, mixed, left, right, state, grad, gz, after, columns):
    fill_columns(columns, [[a[0], a[1]] for a in (left, mixed, right)], 1)
    conv = jnp.dot(weights[1], columns[...], preferred_element_type=f32)
    for n in range(2):
        v, s = gated_sum(conv, n)
        gz[n, :CHANS], gz[n, CHANS:] = gated(grad[n].astype(f32), v, s)
        after[n] = (state[n].astype(f32) + v * s).astype(bf16)


def gated(y, v, s):
    return (y * s).astype(bf16), (y * v * s * (1.0 - s)).astype(bf16)


def whole_line(block, line):
    shift = min(2**block, 2)
    if len(line) == 1:
        units = [line[0][n] for n in range(2 + 2 * shift)]
    else:
        units = [ref[n] for ref in line for n in range(2)]
    return shift, units


def data_kernel(block, weight, gz, left, right, *rest):
    line, (low, tap, columns) = rest[:-3], rest[-3:]
    fill_columns(columns, [[a[0], a[1]] for a in (left, gz, right)], -1)
    grad = jnp.dot(weight[block % 2], columns[...], preferred_element_type=f32)
    shift, units = whole_line(block, line)
    totals = [0.0, 0.0, 0.0]
    for n in range(2):
        m = grad[:, n * CELLS : (n + 1) * CELLS]
        low[n] = m.astype(bf16)
        for which in range(3):
            totals[which] = totals[which] + m * units[n + which * shift].astype(f32)
    for which in range(3):
        tap[:, which : which + 1] = jnp.sum(totals[which], axis=1, keepdims=True)


def weight_kernel(offsets, gz, *rest):
    sources, (out, columns) = rest[:-2], rest[-2:]
    if len(sources) == 2:
        sources, held = sources[:1], sources[1]
        out[:, 128:] = held[...]
    if len(sources) == 1:
        x, t = offsets
        planes = [[sources[0][x + n, t], sources[0][x + n, t + 1]] for n in range(3)]
    else:
        planes = [[a[0], a[1]] for a in sources]
    fill_columns(columns, planes, 1)
    both = jnp.concatenate([gz[0], gz[1]], axis=1)
    order = permutation(lambda r: r % 8 // 4 * 64 + r // 8 * 4 + r % 4)
    both = jnp.dot(order, both, preferred_element_type=f32).astype(bf16)
    grad = lax.dot_general(
        columns[...], both, (((1,), (1,)), ((), ())), preferred_element_type=f32
    )
    out[:13, :128] = grad[: 13 * 128].astype(bf16).reshape(13, 128, 128)
    out[13, :CHANS] = grad[13 * 128 :].astype(bf16)
    out[13, CHANS:128] = jnp.zeros((CHANS, 128), bf16)
    out[14:, :128] = jnp.zeros((2, 128, 128), bf16)


def turned_sum(pieces, start):
    total = pieces[0, start : start + 128].astype(f32)
    for n in range(1, 16):
        total = total + pieces[n, start : start + 128].astype(f32)
    r = lax.broadcasted_iota(jnp.int32, (128, 128), 0)
    c = lax.broadcasted_iota(jnp.int32, (128, 128), 1)
    eye = jnp.where(r == c, 1.0, 0.0).astype(bf16)
    swapped = lax.dot_general(
        eye, total.astype(bf16), (((1,), (1,)), ((), ())), preferred_element_type=f32
    )
    return swapped.astype(bf16)


def halves(value):
    high = value.astype(bf16)
    low = (value - high.astype(f32)).astype(bf16)
    return high, low


def pack_kernel(pieces, taps, out):
    parts = [turned_sum(pieces, start) for start in (0, 384, 256, 128)]
    high, low = halves(taps[...])
    for j in range(16):
        for b in range(BLOCKS):
            out[j, 8 * b : 8 * b + 8] = parts[b][8 * j : 8 * j + 8]
        out[j, 32:40] = high
        out[j, 40:48] = low


def repack_kernel(pieces, out):
    total = pieces[0].astype(f32)
    for n in range(1, 16):
        total = total + pieces[n].astype(f32)
    high, low = halves(total[32:40] + total[40:48])
    grads = total[:32].astype(bf16)
    for p in range(16):
        out[p, :32] = grads
        out[p, 32:40] = high
        out[p, 40:48] = low


def back_state(block, taps, grad, low, behind, ahead):
    shift, units = whole_line(block, (behind, low, ahead)) if block else (1, None)
    if block == 0:
        units = [behind[0], low[0], low[1], ahead[0]]
    t = tap_columns(taps, block)
    return [
        (
            grad[n].astype(f32)
            + t[0] * units[n + 2 * shift].astype(f32)
            + t[1] * units[n + shift].astype(f32)
            + t[2] * units[n].astype(f32)
        ).astype(bf16)
        for n in range(2)
    ]


def last_kernel(block, taps, grad, low, behind, ahead, out):
    for n, g in enumerate(back_state(block, taps, grad, low, behind, ahead)):
        out[n] = g


def step_kernel(block, taps, grad, low, behind, ahead, value, gate, out, gz):
    for n, g in enumerate(back_state(block, taps, grad, low, behind, ahead)):
        out[n] = g
        a, b = gated(g.astype(f32), value[n], gate[n])
        gz[n, :CHANS] = a
        gz[n, CHANS:] = b


def beside(cells, axis, distance):
    count = lax.axis_size(axis)
    pairs = [(i, i + distance) for i in range(count) if 0 <= i + distance < count]
    return lax.ppermute(cells, axis, pairs)


def sides(cells, axis):
    return beside(cells, axis, 1), beside(cells, axis, -1)


def turned(block, distance):
    count = lax.axis_size("phase")
    return lax.ppermute(block, "phase", [((i - distance) % count, i) for i in range(count)])


def neighbours(source, reach):
    if reach == 1:
        return turned(source[1:], 1), turned(source[:1], -1)
    return turned(source, reach // 2), turned(source, -(reach // 2))


def spread(piece, axis):
    count = lax.axis_size(axis)
    copies = jnp.broadcast_to(piece[None], (count,) + piece.shape)
    return lax.all_to_all(copies, axis, 0, 0, tiled=True)


def per_device(frames, temporal_taps, conv_weights, cotangent):
    groups = lax.axis_size("chan")
    own = CHANS // groups
    rows = jnp.transpose(conv_weights, (0, 3, 4, 2, 1)).reshape(BLOCKS, 2 * own, DEPTH)
    taps = temporal_taps.reshape(3 * BLOCKS, CHANS).T
    unit = (2, CHANS, CELLS)
    gunit = (2, 2 * CHANS, CELLS)
    state = jnp.transpose(frames, (1, 0, 2))
    grad = jnp.transpose(cotangent, (1, 0, 2))
    columns = pltpu.VMEM((DEPTH, 2 * CELLS), bf16)
    wide_columns = pltpu.VMEM((2 * DEPTH, 2 * CELLS), bf16)
    place = lax.axis_index("chan")
    edge = jnp.stack([place > 0, place < groups - 1]).astype(f32)
    edge = jnp.broadcast_to(edge[:, None], (2, CELLS))

    odd = lax.axis_index("phase") % 2
    rows = lax.dynamic_slice_in_dim(rows.reshape(2, 4 * own, DEPTH), odd, 1, axis=0)[0]
    mine = spread(rows, "chan")
    count = lax.axis_size("phase")
    other = lax.ppermute(mine, "phase", [(i, i ^ 1) for i in range(count)])
    odd = jnp.broadcast_to(odd.astype(f32), (8, 128))
    weights = [
        call(functools.partial(sort_kernel, n), shaped((2, 128, DEPTH), bf16), odd, mine, other)
        for n in range(2)
    ]

    around = [turned(state[1:], 2), turned(state, 1), state, turned(state, -1)]
    around.append(turned(state[:1], -2))
    line = jnp.concatenate(around)
    cells = [beside(line, "chan", d) for d in (2, 1, -1, -2)]
    cells.insert(2, line)
    mixed0, line0 = call(
        front_mix_kernel,
        [shaped((5, 6, CHANS, CELLS), bf16), shaped((4, CHANS, CELLS), bf16)],
        taps, *cells,
    )
    value0, gate0, line1, mixed1, value1, gate1, state = call(
        front_kernel,
        [
            shaped(unit, f32),
            shaped(unit, f32),
            shaped((6, CHANS, CELLS), bf16),
            shaped((3, 2, CHANS, CELLS), bf16),
            shaped(unit, f32),
            shaped(unit, f32),
            shaped(unit, bf16),
        ],
        edge, taps, weights[0], mixed0, *cells[1:4],
        scratch=[pltpu.VMEM((5, 9 * CHANS, 6 * CELLS), bf16), columns],
    )
    saved = [
        ((line0,), (mixed0,), (1, 2), value0, gate0),
        ((line1,), (mixed1,), (0, 0), value1, gate1),
    ]
    for b in range(2, BLOCKS):
        prior = state
        behind, ahead = neighbours(state, 2**b)
        mixed = call(
            functools.partial(mix_kernel, b), shaped(unit, bf16), taps, state, behind, ahead
        )
        left, right = sides(mixed, "chan")
        if b < BLOCKS - 1:
            value, gate, state = call(
                conv_kernel,
                [shaped(unit, f32), shaped(unit, f32), shaped(unit, bf16)],
                weights[1], mixed, left, right, state,
                scratch=[columns],
            )
        else:
            gz, state = call(
                turn_kernel,
                [shaped(gunit, bf16), shaped(unit, bf16)],
                weights[1], mixed, left, right, state, grad,
                scratch=[columns],
            )
            value = gate = None
        saved.append(((behind, prior, ahead), (left, mixed, right), None, value, gate))
    final = state
    backs = [call(flip_kernel, shaped((2, CHANS, 2 * DEPTH), bf16), w) for w in weights]

    held = []
    tap_grads = [None] * BLOCKS
    for b in reversed(range(BLOCKS)):
        line, mixed, offsets, _, _ = saved[b]
        gleft, gright = sides(gz, "chan")
        extra = [jnp.concatenate(held, axis=1)] if b == 0 else []
        pieces = call(
            functools.partial(weight_kernel, offsets),
            shaped((16, 128 + 384 * len(extra), 128), bf16),
            gz, *mixed, *extra,
            scratch=[columns],
        )
        held.append(pieces)
        if b == 0:
            late = lax.all_to_all(pieces, "phase", 0, 0, tiled=True)
        low, tap_grads[b] = call(
            functools.partial(data_kernel, b),
            [shaped(unit, bf16), shaped((CHANS, 3), f32)],
            backs[b // 2], gz, gleft, gright, *line,
            scratch=[wide_columns],
        )
        behind, ahead = neighbours(low, 2**b)
        if b == 0:
            grad = call(
                functools.partial(last_kernel, b),
                shaped(unit, bf16),
                taps, grad, low, behind, ahead,
            )
        else:
            grad, gz = call(
                functools.partial(step_kernel, b),
                [shaped(unit, bf16), shaped(gunit, bf16)],
                taps, grad, low, behind, ahead, saved[b - 1][3], saved[b - 1][4],
            )
    tap_rows = jnp.concatenate(tap_grads, axis=1).T.reshape(6, 2 * CHANS)
    tap_rows = jnp.pad(tap_rows, [(0, 2), (0, 0)])
    packed = call(pack_kernel, shaped((16, 48, 128), bf16), late, tap_rows)
    packed = lax.all_to_all(packed, "chan", 0, 0, tiled=True)
    packed = call(repack_kernel, shaped((16, 48, 128), bf16), packed)
    packed = lax.all_to_all(packed, "phase", 0, 0, tiled=True)
    grad_rows = packed[:14, :32].astype(f32).reshape(14, BLOCKS, 2, own, 2, CHANS)
    grad_rows = jnp.transpose(grad_rows, (1, 5, 0, 4, 2, 3)).reshape(BLOCKS, CHANS, 28, 2, own)
    grad_weights = grad_rows[:, :, :OFFSETS]
    grad_taps = jnp.sum(packed[:, 32:].astype(f32), axis=0)
    grad_taps = (grad_taps[:6] + grad_taps[8:14]).reshape(BLOCKS, 3, CHANS)
    return (
        jnp.transpose(final, (1, 0, 2)),
        jnp.transpose(grad, (1, 0, 2)),
        grad_taps,
        grad_weights,
    )


def solution(mesh):
    in_specs = (
        P(None, "phase", "chan"),
        P(),
        P(None, None, None, None, "chan"),
        P(None, "phase", "chan"),
    )
    out_specs = (
        P(None, "phase", "chan"),
        P(None, "phase", "chan"),
        P(),
        P(None, None, None, None, "chan"),
    )
    return jax.shard_map(
        per_device, mesh=mesh, in_specs=in_specs, out_specs=out_specs, check_vma=False
    )
```

```python
import functools

import jax
import jax.numpy as jnp
from jax import lax
from jax.experimental import pallas as pl
from jax.experimental.pallas import tpu as pltpu
from jax.sharding import PartitionSpec as P


BLOCKS = 4
SY = 8
SZ = 16
CELLS = SY * SZ
CHANS = 64
OFFSETS = 27
DEPTH = OFFSETS * CHANS
f32 = jnp.float32
bf16 = jnp.bfloat16


def call(body, out_shape, *args, scratch=(), flops=1_000_000, room=12):
    size = sum(a.size * a.dtype.itemsize for a in args)
    return pl.pallas_call(
        body,
        out_shape=out_shape,
        scratch_shapes=list(scratch),
        compiler_params=pltpu.CompilerParams(vmem_limit_bytes=room << 20),
        cost_estimate=pl.CostEstimate(flops=flops, bytes_accessed=size, transcendentals=0),
    )(*args)


def shaped(shape, kind):
    return jax.ShapeDtypeStruct(shape, kind)


def inside_masks(sign):
    places = lax.broadcasted_iota(jnp.int32, (1, CELLS), 1)
    masks = []
    for kk in range(9):
        dy, dz = sign * (kk // 3 - 1), sign * (kk % 3 - 1)
        y, z = places // SZ + dy, places % SZ + dz
        masks.append((y >= 0) & (y < SY) & (z >= 0) & (z < SZ))
    return masks


def spread_unit(unit, masks, sign):
    wide = unit.astype(f32)
    pieces = []
    for kk in range(9):
        step = sign * ((kk // 3 - 1) * SZ + kk % 3 - 1)
        if step == 0:
            pieces.append(unit)
        else:
            moved = pltpu.roll(wide, (-step) % CELLS, 1)
            pieces.append(jnp.where(masks[kk], moved, 0.0).astype(bf16))
    return pieces


def fill_columns(columns, planes, sign):
    masks = inside_masks(sign)
    rows = planes[0][0].shape[0]
    for dx in range(3):
        source = planes[dx] if sign > 0 else planes[2 - dx]
        for t, unit in enumerate(source):
            for kk, piece in enumerate(spread_unit(unit, masks, sign)):
                start = (dx * 9 + kk) * rows
                columns[start : start + rows, t * CELLS : (t + 1) * CELLS] = piece


def permutation(wanted):
    r = lax.broadcasted_iota(jnp.int32, (128, 128), 0)
    c = lax.broadcasted_iota(jnp.int32, (128, 128), 1)
    return jnp.where(wanted(r) == c, 1.0, 0.0).astype(bf16)


def sort_kernel(half, odd, mine, other, out):
    order = permutation(lambda r: r % 64 // 4 * 8 + r // 64 * 4 + r % 4)
    keep = (odd[:1, :1] > 0.5) if half else (odd[:1, :1] < 0.5)
    for n in range(2):
        here = mine[:, 8 * n : 8 * n + 8, :].reshape(128, DEPTH)
        there = other[:, 8 * n : 8 * n + 8, :].reshape(128, DEPTH)
        rows = jnp.where(keep, here.astype(f32), there.astype(f32)).astype(bf16)
        out[n] = jnp.dot(order, rows, preferred_element_type=f32).astype(bf16)


def flip_kernel(weights, out):
    r = lax.broadcasted_iota(jnp.int32, (CHANS, CHANS), 0)
    c = lax.broadcasted_iota(jnp.int32, (CHANS, CHANS), 1)
    eye = jnp.where(r == c, 1.0, 0.0).astype(bf16)
    for n in range(2):
        for k in range(OFFSETS):
            piece = weights[n, :, k * CHANS : (k + 1) * CHANS]
            turned = lax.dot_general(
                eye, piece, (((1,), (1,)), ((), ())), preferred_element_type=f32
            )
            out[n, :, k * 128 : (k + 1) * 128] = turned.astype(bf16)


def tap_columns(taps, block):
    return [taps[:, 3 * block + n : 3 * block + n + 1] for n in range(3)]


def mix(t, before, now, after):
    total = t[0] * before.astype(f32) + t[1] * now.astype(f32) + t[2] * after.astype(f32)
    return total.astype(bf16)


def mix_kernel(block, taps, state, behind, ahead, out):
    t = tap_columns(taps, block)
    for n in range(2):
        out[n] = mix(t, behind[n], state[n], ahead[n])


def wide_columns(columns, planes):
    masks = inside_masks(1)
    for x, units in enumerate(planes):
        for q, unit in enumerate(units):
            for kk, piece in enumerate(spread_unit(unit, masks, 1)):
                columns[x, kk * CHANS : (kk + 1) * CHANS, q * CELLS : (q + 1) * CELLS] = piece


def wide_conv(weight, columns, x):
    third = 9 * CHANS
    total = None
    for dx in range(3):
        part = jnp.dot(
            weight[:, dx * third : (dx + 1) * third], columns[x + dx], preferred_element_type=f32
        )
        total = part if dx == 0 else total + part
    return total


def front_mix_kernel(taps, *refs):
    planes, (mixed, line) = refs[:5], refs[5:]
    t = tap_columns(taps, 0)
    for x in range(5):
        for q in range(6):
            mixed[x, q] = mix(t, planes[x][q], planes[x][q + 1], planes[x][q + 2])
    for q in range(4):
        line[q] = planes[2][q + 2]


def gated_sum(conv, n):
    v = conv[:CHANS, n * CELLS : (n + 1) * CELLS]
    s = jax.nn.sigmoid(conv[CHANS:, n * CELLS : (n + 1) * CELLS])
    return v, s


def front_kernel(
    edge, taps, weights, mixed, before, own, after_own,
    value0, gate0, line1, mixed1, value1, gate1, after, columns, narrow,
):
    wide_columns(columns, [[mixed[x, q] for q in range(6)] for x in range(5)])
    t = tap_columns(taps, 1)
    planes = []
    for x in range(3):
        conv = wide_conv(weights[0], columns, x)
        f = (before, own, after_own)[x]
        states = []
        for q in range(6):
            v, s = gated_sum(conv, q)
            state = f[q + 1].astype(f32) + v * s
            if x == 1:
                state = state.astype(bf16)
                line1[q] = state
                if q in (2, 3):
                    value0[q - 2] = v
                    gate0[q - 2] = s
            else:
                flag = edge[x // 2 : x // 2 + 1, :] > 0.5
                state = jnp.where(flag, state, 0.0).astype(bf16)
            states.append(state)
        units = [mix(t, states[n], states[n + 2], states[n + 4]) for n in range(2)]
        for n in range(2):
            mixed1[x, n] = units[n]
        planes.append(units)
    fill_columns(narrow, planes, 1)
    conv = jnp.dot(weights[1], narrow[...], preferred_element_type=f32)
    for n in range(2):
        v, s = gated_sum(conv, n)
        value1[n] = v
        gate1[n] = s
        after[n] = (line1[n + 2].astype(f32) + v * s).astype(bf16)


def conv_kernel(weights, mixed, left, right, state, value, gate, after, columns):
    fill_columns(columns, [[a[0], a[1]] for a in (left, mixed, right)], 1)
    conv = jnp.dot(weights[0], columns[...], preferred_element_type=f32)
    for n in range(2):
        v, s = gated_sum(conv, n)
        value[n] = v
        gate[n] = s
        after[n] = (state[n].astype(f32) + v * s).astype(bf16)


def turn_kernel(weights, mixed, left, right, state, grad, gz, after, columns):
    fill_columns(columns, [[a[0], a[1]] for a in (left, mixed, right)], 1)
    conv = jnp.dot(weights[1], columns[...], preferred_element_type=f32)
    for n in range(2):
        v, s = gated_sum(conv, n)
        gz[n, :CHANS], gz[n, CHANS:] = gated(grad[n].astype(f32), v, s)
        after[n] = (state[n].astype(f32) + v * s).astype(bf16)


def gated(y, v, s):
    return (y * s).astype(bf16), (y * v * s * (1.0 - s)).astype(bf16)


def whole_line(block, line):
    shift = min(2**block, 2)
    if len(line) == 1:
        units = [line[0][n] for n in range(2 + 2 * shift)]
    else:
        units = [ref[n] for ref in line for n in range(2)]
    return shift, units


def data_kernel(block, weight, gz, left, right, *rest):
    line, (low, tap, columns) = rest[:-3], rest[-3:]
    fill_columns(columns, [[a[0], a[1]] for a in (left, gz, right)], -1)
    grad = jnp.dot(weight[block % 2], columns[...], preferred_element_type=f32)
    shift, units = whole_line(block, line)
    totals = [0.0, 0.0, 0.0]
    for n in range(2):
        m = grad[:, n * CELLS : (n + 1) * CELLS]
        low[n] = m.astype(bf16)
        for which in range(3):
            totals[which] = totals[which] + m * units[n + which * shift].astype(f32)
    for which in range(3):
        tap[:, which : which + 1] = jnp.sum(totals[which], axis=1, keepdims=True)


def weight_product(gz, planes, columns):
    fill_columns(columns, planes, 1)
    both = jnp.concatenate([gz[0], gz[1]], axis=1)
    order = permutation(lambda r: r % 8 // 4 * 64 + r // 8 * 4 + r % 4)
    both = jnp.dot(order, both, preferred_element_type=f32).astype(bf16)
    grad = lax.dot_general(
        columns[...], both, (((1,), (1,)), ((), ())), preferred_element_type=f32
    )
    grad = grad.astype(bf16)
    pieces = [grad[n * 128 : (n + 1) * 128] for n in range(13)]
    pieces.append(jnp.concatenate([grad[13 * 128 :], jnp.zeros((CHANS, 128), bf16)], axis=0))
    return pieces + [jnp.zeros((128, 128), bf16)] * 2


def weight_kernel(offsets, gz, *rest):
    sources, (out, columns) = rest[:-2], rest[-2:]
    if len(sources) == 1:
        x, t = offsets
        planes = [[sources[0][x + n, t], sources[0][x + n, t + 1]] for n in range(3)]
    else:
        planes = [[a[0], a[1]] for a in sources]
    for n, piece in enumerate(weight_product(gz, planes, columns)):
        out[n] = piece


def last_weight_kernel(offsets, odd, gz, mixed, held3, held2, held1, keep, send, columns):
    x, t = offsets
    planes = [[mixed[x + n, t], mixed[x + n, t + 1]] for n in range(3)]
    pieces = weight_product(gz, planes, columns)
    mine = odd[:1, :1] > 0.5
    for m in range(8):
        pairs = [(pieces[2 * m], pieces[2 * m + 1])]
        pairs += [(held[2 * m], held[2 * m + 1]) for held in (held1, held2, held3)]
        for b, (even_part, odd_part) in enumerate(pairs):
            lower, upper = even_part.astype(f32), odd_part.astype(f32)
            rows = slice(128 * b, 128 * b + 128)
            keep[m, rows] = jnp.where(mine, upper, lower).astype(bf16)
            send[m, rows] = jnp.where(mine, lower, upper).astype(bf16)


def join_kernel(keep, other, out):
    out[...] = (keep[...].astype(f32) + other[...].astype(f32)).astype(bf16)


def turned_sum(pieces, start):
    total = pieces[0, start : start + 128].astype(f32)
    for n in range(1, 8):
        total = total + pieces[n, start : start + 128].astype(f32)
    r = lax.broadcasted_iota(jnp.int32, (128, 128), 0)
    c = lax.broadcasted_iota(jnp.int32, (128, 128), 1)
    eye = jnp.where(r == c, 1.0, 0.0).astype(bf16)
    swapped = lax.dot_general(
        eye, total.astype(bf16), (((1,), (1,)), ((), ())), preferred_element_type=f32
    )
    return swapped.astype(bf16)


def halves(value):
    high = value.astype(bf16)
    low = (value - high.astype(f32)).astype(bf16)
    return high, low


def pack_kernel(pieces, taps, out):
    parts = [turned_sum(pieces, 128 * b) for b in range(BLOCKS)]
    high, low = halves(taps[...])
    for j in range(16):
        for b in range(BLOCKS):
            out[j, 8 * b : 8 * b + 8] = parts[b][8 * j : 8 * j + 8]
        out[j, 32:40] = high
        out[j, 40:48] = low


def repack_kernel(pieces, out):
    total = pieces[0].astype(f32)
    for n in range(1, 16):
        total = total + pieces[n].astype(f32)
    high, low = halves(total[32:40] + total[40:48])
    grads = total[:32].astype(bf16)
    for p in range(16):
        out[p, :32] = grads
        out[p, 32:40] = high
        out[p, 40:48] = low


def back_state(block, taps, grad, low, behind, ahead):
    shift, units = whole_line(block, (behind, low, ahead)) if block else (1, None)
    if block == 0:
        units = [behind[0], low[0], low[1], ahead[0]]
    t = tap_columns(taps, block)
    return [
        (
            grad[n].astype(f32)
            + t[0] * units[n + 2 * shift].astype(f32)
            + t[1] * units[n + shift].astype(f32)
            + t[2] * units[n].astype(f32)
        ).astype(bf16)
        for n in range(2)
    ]


def last_kernel(block, taps, grad, low, behind, ahead, out):
    for n, g in enumerate(back_state(block, taps, grad, low, behind, ahead)):
        out[n] = g


def step_kernel(block, taps, grad, low, behind, ahead, value, gate, out, gz):
    for n, g in enumerate(back_state(block, taps, grad, low, behind, ahead)):
        out[n] = g
        a, b = gated(g.astype(f32), value[n], gate[n])
        gz[n, :CHANS] = a
        gz[n, CHANS:] = b


def beside(cells, axis, distance):
    count = lax.axis_size(axis)
    pairs = [(i, i + distance) for i in range(count) if 0 <= i + distance < count]
    return lax.ppermute(cells, axis, pairs)


def sides(cells, axis):
    return beside(cells, axis, 1), beside(cells, axis, -1)


def turned(block, distance):
    count = lax.axis_size("phase")
    return lax.ppermute(block, "phase", [((i - distance) % count, i) for i in range(count)])


def neighbours(source, reach):
    if reach == 1:
        return turned(source[1:], 1), turned(source[:1], -1)
    return turned(source, reach // 2), turned(source, -(reach // 2))


def spread(piece, axis):
    count = lax.axis_size(axis)
    copies = jnp.broadcast_to(piece[None], (count,) + piece.shape)
    return lax.all_to_all(copies, axis, 0, 0, tiled=True)


def per_device(frames, temporal_taps, conv_weights, cotangent):
    groups = lax.axis_size("chan")
    own = CHANS // groups
    rows = jnp.transpose(conv_weights, (0, 3, 4, 2, 1)).reshape(BLOCKS, 2 * own, DEPTH)
    taps = temporal_taps.reshape(3 * BLOCKS, CHANS).T
    unit = (2, CHANS, CELLS)
    gunit = (2, 2 * CHANS, CELLS)
    state = jnp.transpose(frames, (1, 0, 2))
    grad = jnp.transpose(cotangent, (1, 0, 2))
    columns = pltpu.VMEM((DEPTH, 2 * CELLS), bf16)
    wide_columns = pltpu.VMEM((2 * DEPTH, 2 * CELLS), bf16)
    place = lax.axis_index("chan")
    edge = jnp.stack([place > 0, place < groups - 1]).astype(f32)
    edge = jnp.broadcast_to(edge[:, None], (2, CELLS))

    odd = lax.axis_index("phase") % 2
    rows = lax.dynamic_slice_in_dim(rows.reshape(2, 4 * own, DEPTH), odd, 1, axis=0)[0]
    mine = spread(rows, "chan")
    count = lax.axis_size("phase")
    other = lax.ppermute(mine, "phase", [(i, i ^ 1) for i in range(count)])
    odd = jnp.broadcast_to(odd.astype(f32), (8, 128))
    weights = [
        call(functools.partial(sort_kernel, n), shaped((2, 128, DEPTH), bf16), odd, mine, other)
        for n in range(2)
    ]

    around = [turned(state[1:], 2), turned(state, 1), state, turned(state, -1)]
    around.append(turned(state[:1], -2))
    line = jnp.concatenate(around)
    cells = [beside(line, "chan", d) for d in (2, 1, -1, -2)]
    cells.insert(2, line)
    mixed0, line0 = call(
        front_mix_kernel,
        [shaped((5, 6, CHANS, CELLS), bf16), shaped((4, CHANS, CELLS), bf16)],
        taps, *cells,
    )
    value0, gate0, line1, mixed1, value1, gate1, state = call(
        front_kernel,
        [
            shaped(unit, f32),
            shaped(unit, f32),
            shaped((6, CHANS, CELLS), bf16),
            shaped((3, 2, CHANS, CELLS), bf16),
            shaped(unit, f32),
            shaped(unit, f32),
            shaped(unit, bf16),
        ],
        edge, taps, weights[0], mixed0, *cells[1:4],
        scratch=[pltpu.VMEM((5, 9 * CHANS, 6 * CELLS), bf16), columns],
    )
    saved = [
        ((line0,), (mixed0,), (1, 2), value0, gate0),
        ((line1,), (mixed1,), (0, 0), value1, gate1),
    ]
    for b in range(2, BLOCKS):
        prior = state
        behind, ahead = neighbours(state, 2**b)
        mixed = call(
            functools.partial(mix_kernel, b), shaped(unit, bf16), taps, state, behind, ahead
        )
        left, right = sides(mixed, "chan")
        if b < BLOCKS - 1:
            value, gate, state = call(
                conv_kernel,
                [shaped(unit, f32), shaped(unit, f32), shaped(unit, bf16)],
                weights[1], mixed, left, right, state,
                scratch=[columns],
            )
        else:
            gz, state = call(
                turn_kernel,
                [shaped(gunit, bf16), shaped(unit, bf16)],
                weights[1], mixed, left, right, state, grad,
                scratch=[columns],
            )
            value = gate = None
        saved.append(((behind, prior, ahead), (left, mixed, right), None, value, gate))
    final = state
    backs = [call(flip_kernel, shaped((2, CHANS, 2 * DEPTH), bf16), w) for w in weights]

    held = []
    tap_grads = [None] * BLOCKS
    for b in reversed(range(BLOCKS)):
        line, mixed, offsets, _, _ = saved[b]
        gleft, gright = sides(gz, "chan")
        if b > 0:
            pieces = call(
                functools.partial(weight_kernel, offsets),
                shaped((16, 128, 128), bf16),
                gz, *mixed,
                scratch=[columns],
            )
            held.append(pieces)
        else:
            keep, send = call(
                functools.partial(last_weight_kernel, offsets),
                [shaped((8, 512, 128), bf16)] * 2,
                odd, gz, *mixed, *held,
                scratch=[columns],
                room=16,
            )
        if b == 0:
            other = lax.ppermute(send, "phase", [(i, i ^ 1) for i in range(count)])
            late = call(join_kernel, shaped((8, 512, 128), bf16), keep, other)
            alike = [list(range(n, count, 2)) for n in range(2)]
            late = lax.all_to_all(
                late, "phase", 0, 0, tiled=True, axis_index_groups=alike
            )
        low, tap_grads[b] = call(
            functools.partial(data_kernel, b),
            [shaped(unit, bf16), shaped((CHANS, 3), f32)],
            backs[b // 2], gz, gleft, gright, *line,
            scratch=[wide_columns],
        )
        behind, ahead = neighbours(low, 2**b)
        if b == 0:
            grad = call(
                functools.partial(last_kernel, b),
                shaped(unit, bf16),
                taps, grad, low, behind, ahead,
            )
        else:
            grad, gz = call(
                functools.partial(step_kernel, b),
                [shaped(unit, bf16), shaped(gunit, bf16)],
                taps, grad, low, behind, ahead, saved[b - 1][3], saved[b - 1][4],
            )
    tap_rows = jnp.concatenate(tap_grads, axis=1).T.reshape(6, 2 * CHANS)
    tap_rows = jnp.pad(tap_rows, [(0, 2), (0, 0)])
    packed = call(pack_kernel, shaped((16, 48, 128), bf16), late, tap_rows)
    packed = lax.all_to_all(packed, "chan", 0, 0, tiled=True)
    packed = call(repack_kernel, shaped((16, 48, 128), bf16), packed)
    packed = lax.all_to_all(packed, "phase", 0, 0, tiled=True)
    grad_rows = packed[:14, :32].astype(f32).reshape(14, BLOCKS, 2, own, 2, CHANS)
    grad_rows = jnp.transpose(grad_rows, (1, 5, 0, 4, 2, 3)).reshape(BLOCKS, CHANS, 28, 2, own)
    grad_weights = grad_rows[:, :, :OFFSETS]
    grad_taps = jnp.sum(packed[:, 32:].astype(f32), axis=0)
    grad_taps = (grad_taps[:6] + grad_taps[8:14]).reshape(BLOCKS, 3, CHANS)
    return (
        jnp.transpose(final, (1, 0, 2)),
        jnp.transpose(grad, (1, 0, 2)),
        grad_taps,
        grad_weights,
    )


def solution(mesh):
    in_specs = (
        P(None, "phase", "chan"),
        P(),
        P(None, None, None, None, "chan"),
        P(None, "phase", "chan"),
    )
    out_specs = (
        P(None, "phase", "chan"),
        P(None, "phase", "chan"),
        P(),
        P(None, None, None, None, "chan"),
    )
    return jax.shard_map(
        per_device, mesh=mesh, in_specs=in_specs, out_specs=out_specs, check_vma=False
    )
```
